32 devices in a mesh: row: 4 (over x, core), col: 8 (over z, y).
Axes of the slice: x: 2, y: 2, z: 4, core: 2. Of those that a mesh axis runs over, the one named last changes fastest.
Arguments:
- matrix: float32 [6144, 12288], P('row', 'col'), may hold values from -6 to 6
- far_diag: float32 [4, 1536], P('row'), may hold values from -6 to 6
- vectors: float32 [12288, 128], P(('row', 'col'))
- factors: float32 [128, 128], replicated, may hold values from -0.5 to 0.5
Outputs:
- updated: float32 [6144, 12288], P('row', 'col')
- far_updated: float32 [4, 1536], P('row')
The draws below stay inside these ranges and needn't reach their ends.
All inputs are finite; a program needn't handle non-finite values.
Results may differ from the reference program's by a relative error of at most 0.0003.
Values sent between devices are 32-bit elements; how exact they have to be, the bound alone decides.
No kernel may reach another device: no remote copies, remote signals or barrier semaphores. Data moves between devices by JAX's collectives and lax.ppermute only.
A program may use at most 128 MiB of HBM per device.

```python
import jax
import jax.numpy as jnp
from jax import lax

TILE = 1536
NB = 128
GRID = 8
HALF = 4
N = 12288


def draw_vectors(key, part):
    spread = (N * NB) ** (-0.25)
    return spread * jax.random.normal(key, (N, NB), jnp.float32)


def level_of(stream_key, dims, shards, low, high):
    def one(dim, parts):
        steps = jax.random.uniform(jax.random.fold_in(jax.random.fold_in(stream_key, 6), dim), (parts,), jnp.float32, low / len(shards), high / len(shards))
        return jnp.repeat(jnp.exp(steps), dims[dim] // parts).reshape((-1,) + (1,) * (len(dims) - dim - 1))

    level = one(*shards[0])
    for cut in shards[1:]:
        level = level * one(*cut)
    return level


def bell_draw(own_key, extent, deviation, most, split=(), dtype=jnp.bfloat16):
    drawn = jax.random.normal(own_key, extent, jnp.float32) * deviation
    if len(split) > 0:
        drawn = level_of(own_key, extent, split, -0.22, 0.18) * drawn
    return jnp.clip(drawn, min=-most, max=most).astype(dtype)


def setup_inputs(seed: int = 0) -> dict:
    seeds = jax.random.split(jax.random.key(seed), 5)
    matrix = bell_draw(seeds[0], (HALF * TILE, GRID * TILE), 1.0, 6.0, ((0, 4), (1, 8)), jnp.float32)
    far_diag = bell_draw(seeds[1], (HALF, TILE), 1.0, 6.0, ((0, 4),), jnp.float32)
    vectors = draw_vectors(jax.random.fold_in(seeds[4], 71), 0)
    factors = bell_draw(seeds[3], (NB, NB), NB ** -0.5, 0.5, (), jnp.float32)
    return dict(matrix=matrix, far_diag=far_diag, vectors=vectors, factors=factors)


def product(left, right):
    return jnp.dot(left, right, preferred_element_type=jnp.float32, precision=lax.Precision.HIGHEST)


def sym_pair(block, low_diag):
    lower_part = jnp.tril(block)
    lead_full = lower_part + jnp.tril(block, -1).T
    upper_part = jnp.triu(block, 1)
    other_full = upper_part + upper_part.T + jnp.diag(low_diag)
    return lead_full, other_full


def tile_pair(row_at, col_at):
    far_row = GRID - 1 - row_at
    if col_at < row_at:
        return row_at, col_at
    if col_at == row_at:
        return row_at, far_row
    return far_row, col_at - row_at - 1


def reference(matrix, far_diag, vectors, factors):
    def block(row_at, col_at):
        return matrix[row_at * TILE:(row_at + 1) * TILE, col_at * TILE:(col_at + 1) * TILE]

    def vpart(index):
        return vectors[index * TILE:(index + 1) * TILE]

    zparts = [jnp.zeros((TILE, NB), jnp.float32) for index in range(GRID)]
    for row_at in range(HALF):
        for col_at in range(GRID):
            lead, other = tile_pair(row_at, col_at)
            tile_now = block(row_at, col_at)
            if col_at == row_at:
                lead_full, other_full = sym_pair(tile_now, far_diag[row_at])
                zparts[lead] = zparts[lead] + product(lead_full, vpart(lead))
                zparts[other] = zparts[other] + product(other_full, vpart(other))
            else:
                zparts[lead] = zparts[lead] + product(tile_now, vpart(other))
                zparts[other] = zparts[other] + product(tile_now.T, vpart(lead))
    zvals = jnp.concatenate(zparts, axis=0)
    gram_sum = product(vectors.T, zvals)
    middle = product(product(factors.T, gram_sum), factors)
    wvals = product(zvals, factors) - 0.5 * product(vectors, middle)

    def wpart(index):
        return wvals[index * TILE:(index + 1) * TILE]

    def change(lead, other):
        left = jnp.concatenate([vpart(lead), wpart(lead)], axis=1)
        right = jnp.concatenate([wpart(other), vpart(other)], axis=1)
        return product(left, right.T)

    row_blocks = []
    far_rows = []
    for row_at in range(HALF):
        pieces = []
        for col_at in range(GRID):
            lead, other = tile_pair(row_at, col_at)
            tile_now = block(row_at, col_at)
            if col_at == row_at:
                lead_full, other_full = sym_pair(tile_now, far_diag[row_at])
                lead_new = lead_full - change(lead, lead)
                other_new = other_full - change(other, other)
                pieces.append(jnp.tril(lead_new) + jnp.triu(other_new, 1))
            else:
                pieces.append(tile_now - change(lead, other))
        row_blocks.append(jnp.concatenate(pieces, axis=1))
        far_row = GRID - 1 - row_at
        far_rows.append(far_diag[row_at] - 2.0 * jnp.sum(vpart(far_row) * wpart(far_row), axis=1))
    return jnp.concatenate(row_blocks, axis=0), jnp.stack(far_rows, axis=0)
```

```python
import functools

import jax
import jax.numpy as jnp
import numpy as np
from jax import lax
from jax.experimental import pallas as pl
from jax.experimental.pallas import tpu as pltpu
from jax.sharding import PartitionSpec as P

AXES = ("row", "col")
F32 = jnp.float32
BF16 = jnp.bfloat16


def tile_pair(grid, h, k):
    if k < h:
        return h, k
    if k == h:
        return h, grid - 1 - h
    return grid - 1 - h, k - h - 1


def make_flows(half, grid):
    pieces = half
    flows = []
    for h in range(half):
        for k in range(grid):
            for role, tile in enumerate(tile_pair(grid, h, k)):
                for piece in range(pieces):
                    flows.append((tile * pieces + piece, h * grid + k, role * pieces + piece))
    return flows


def color_flows(flows, count):
    left = list(flows)
    rounds = []
    for _ in range(len(flows) // count):
        out_of = [[] for _ in range(count)]
        for index, flow in enumerate(left):
            out_of[flow[0]].append(index)
        match = [-1] * count

        def augment(home, seen):
            for index in out_of[home]:
                member = left[index][1]
                if member in seen:
                    continue
                seen.add(member)
                if match[member] < 0 or augment(left[match[member]][0], seen):
                    match[member] = index
                    return True
            return False

        for home in range(count):
            assert augment(home, set())
        rounds.append([left[index] for index in match])
        used = set(match)
        left = [flow for index, flow in enumerate(left) if index not in used]
    return rounds


def split(value):
    high = value.astype(BF16)
    return high, (value - high.astype(F32)).astype(BF16)


def dot(left, right):
    return jnp.dot(left, right, preferred_element_type=F32)


def dot_nt(left, right):
    return lax.dot_general(left, right, (((1,), (1,)), ((), ())), preferred_element_type=F32)


def dot3(left, right):
    lh, ll = split(left)
    rh, rl = split(right)
    return dot(lh, rh) + (dot(lh, rl) + dot(ll, rh))


def z_kernel(n_rounds, step, slots, flags, a_ref, d_ref, *refs):
    v_in = refs[:n_rounds]
    z_out = refs[n_rounds:2 * n_rounds]
    g_out, v_out = refs[2 * n_rounds:2 * n_rounds + 2]
    vcat, vt_hi, vt_lo, x_acc, zt_acc = refs[2 * n_rounds + 2:]
    tile = a_ref.shape[1]
    nb = v_in[0].shape[1]
    rows = v_in[0].shape[0]
    count = tile // step
    p = pl.program_id(0)
    diag = flags[0] == 1

    @pl.when(p == 0)
    def _():
        per = tile // rows
        for r in range(n_rounds):
            slot = slots[r]
            role = slot // per
            at = pl.multiple_of((slot % per) * rows, rows)
            v_out[role, pl.ds(at, rows), :] = v_in[r][...]
        for role in range(2):
            for b in range(count):
                cut = slice(b * step, (b + 1) * step)
                v = v_out[role, cut, :]
                vh, vl = split(v)
                vcat[role, cut, 0:nb] = vh
                vcat[role, cut, nb:2 * nb] = vl
                vth, vtl = split(v.T)
                vt_hi[role, :, cut] = vth
                vt_lo[role, :, cut] = vtl
        x_acc[...] = jnp.zeros_like(x_acc)
        zt_acc[...] = jnp.zeros_like(zt_acc)

    p_at = pl.multiple_of(p * step, step)

    def row_part(block, r_role, x_role, q):
        bh, bl = split(block)
        rhs = vcat[r_role, q * step:(q + 1) * step, :]
        both = dot(bh, rhs)
        x_acc[x_role, pl.ds(p_at, step), :] += both[:, :nb] + (both[:, nb:] + dot(bl, rhs[:, :nb]))
        return bh, bl

    def col_part(bh, bl, s_role, y_role, q):
        vth = vt_hi[s_role, :, pl.ds(p_at, step)]
        vtl = vt_lo[s_role, :, pl.ds(p_at, step)]
        zt_acc[y_role, :, q * step:(q + 1) * step] += dot(vth, bh) + (dot(vtl, bh) + dot(vth, bl))

    for q in range(count):
        block = a_ref[:, q * step:(q + 1) * step]

        @pl.when(p != q)
        def _():
            side = jnp.where(q < p, 0, 1)
            bh, bl = row_part(block, jnp.where(diag, side, 1), jnp.where(diag, side, 0), q)
            col_part(bh, bl, jnp.where(diag, side, 0), jnp.where(diag, side, 1), q)

        @pl.when((p == q) & jnp.logical_not(diag))
        def _():
            bh, bl = row_part(block, 1, 0, q)
            col_part(bh, bl, 0, 1, q)

        @pl.when((p == q) & diag)
        def _():
            at_row = lax.broadcasted_iota(jnp.int32, (step, step), 0)
            at_col = lax.broadcasted_iota(jnp.int32, (step, step), 1)
            flip = block.T
            first = jnp.where(at_row >= at_col, block, flip)
            far = d_ref[0:1, q * step:(q + 1) * step]
            second = jnp.where(at_row < at_col, block, jnp.where(at_row > at_col, flip, far))
            row_part(first, 0, 0, q)
            row_part(second, 1, 1, q)

    @pl.when(p == count - 1)
    def _():
        for role in range(2):
            x_acc[role] += zt_acc[role].T
        gram = jnp.zeros((nb, nb), F32)
        for role in range(2):
            zh, zl = split(x_acc[role])
            gram += dot(vt_hi[role], zh) + (dot(vt_lo[role], zh) + dot(vt_hi[role], zl))
        g_out[...] = gram
        per = tile // rows
        for r in range(n_rounds):
            slot = slots[r]
            z_out[r][...] = x_acc[slot // per, pl.ds(pl.multiple_of((slot % per) * rows, rows), rows), :]


def w_kernel(n_rounds, slots, flags, v_ref, g_ref, t_ref, d_ref, *refs):
    z_in = refs[:n_rounds]
    hi_out, lo_out, far_out = refs[n_rounds:n_rounds + 3]
    w_acc = refs[n_rounds + 3]
    rows, nb = z_in[0].shape
    tile = v_ref.shape[1]
    per = tile // rows
    factors = t_ref[...]
    middle = dot3(dot3(factors.T, g_ref[...]), factors)
    half_mid = -0.5 * middle
    for r in range(n_rounds):
        slot = slots[r]
        role = slot // per
        at = pl.multiple_of((slot % per) * rows, rows)
        v = v_ref[role, pl.ds(at, rows), :]
        w = dot3(z_in[r][...], factors) + dot3(v, half_mid)
        vh, vl = split(v)
        wh, wl = split(w)
        w_acc[role, pl.ds(at, rows), :] = w
        hi_out[role, pl.ds(at, rows), 0:nb] = vh
        hi_out[role, pl.ds(at, rows), nb:2 * nb] = wh
        lo_out[role, pl.ds(at, rows), 0:nb] = vl
        lo_out[role, pl.ds(at, rows), nb:2 * nb] = wl
    far_role = flags[1]
    prod = v_ref[far_role] * w_acc[far_role]
    total = jnp.sum(prod.T, axis=0, keepdims=True)
    far_out[...] = d_ref[...] - 2.0 * total


def u_kernel(step, slots, flags, a_ref, hi_ref, lo_ref, out_ref, qh_ref, ql_ref):
    tile = a_ref.shape[1]
    nb = hi_ref.shape[2] // 2
    count = tile // step
    p = pl.program_id(0)
    diag = flags[0] == 1
    p_at = pl.multiple_of(p * step, step)

    @pl.when(p == 0)
    def _():
        for role in range(2):
            qh_ref[role, :, 0:nb] = hi_ref[role, :, nb:2 * nb]
            qh_ref[role, :, nb:2 * nb] = hi_ref[role, :, 0:nb]
            ql_ref[role, :, 0:nb] = lo_ref[role, :, nb:2 * nb]
            ql_ref[role, :, nb:2 * nb] = lo_ref[role, :, 0:nb]

    def change(left, right, q):
        cut = slice(q * step, (q + 1) * step)
        ph = hi_ref[left, pl.ds(p_at, step), :]
        plo = lo_ref[left, pl.ds(p_at, step), :]
        qh = qh_ref[right, cut, :]
        ql = ql_ref[right, cut, :]
        return dot_nt(ph, qh) + (dot_nt(ph, ql) + dot_nt(plo, qh))

    for q in range(count):
        cut = slice(q * step, (q + 1) * step)

        @pl.when((p != q) | jnp.logical_not(diag))
        def _():
            side = jnp.where(q < p, 0, 1)
            out_ref[:, cut] = a_ref[:, cut] - change(
                jnp.where(diag, side, 0), jnp.where(diag, side, 1), q
            )

        @pl.when((p == q) & diag)
        def _():
            at_row = lax.broadcasted_iota(jnp.int32, (step, step), 0)
            at_col = lax.broadcasted_iota(jnp.int32, (step, step), 1)
            out_ref[:, cut] = a_ref[:, cut] - jnp.where(
                at_row >= at_col, change(0, 0, q), change(1, 1, q)
            )


def solution(mesh):
    half, grid = mesh.shape["row"], mesh.shape["col"]
    count = half * grid
    rounds = color_flows(make_flows(half, grid), count)
    n_rounds = len(rounds)
    slot_table = np.zeros((count, n_rounds), np.int32)
    for r, flows in enumerate(rounds):
        for _, member, slot in flows:
            slot_table[member, r] = slot
    down = [[(home, member) for home, member, _ in flows] for flows in rounds]
    up = [[(member, home) for home, member, _ in flows] for flows in rounds]
    far_perm = [
        (h * grid + k + h, h * grid + k) for h in range(half) for k in range(h)
    ]

    def all_sum(value):
        gap = 1
        while gap < count:
            perm = [(d, d ^ gap) for d in range(count)]
            value = value + lax.ppermute(value, AXES, perm)
            gap *= 2
        return value

    def body(matrix, far_diag, vectors, factors):
        tile = matrix.shape[0]
        rows, nb = vectors.shape
        step = tile // 3 if tile % 384 == 0 else tile
        row_at = lax.axis_index("row")
        col_at = lax.axis_index("col")
        me = row_at * grid + col_at
        slots = lax.dynamic_slice_in_dim(jnp.asarray(slot_table), me, 1, 0)[0]
        flags = jnp.stack(
            [(col_at == row_at).astype(jnp.int32), (col_at == row_at).astype(jnp.int32)]
        )
        v_in = [lax.ppermute(vectors, AXES, perm) for perm in down]
        whole = lambda *shape: pl.BlockSpec(shape, lambda p, *_: (0,) * len(shape))
        strip = pl.BlockSpec((step, tile), lambda p, *_: (p, 0))
        piece = jax.ShapeDtypeStruct((rows, nb), F32)

        outs = pl.pallas_call(
            functools.partial(z_kernel, n_rounds, step),
            out_shape=[piece] * n_rounds
            + [jax.ShapeDtypeStruct((nb, nb), F32), jax.ShapeDtypeStruct((2, tile, nb), F32)],
            grid_spec=pltpu.PrefetchScalarGridSpec(
                num_scalar_prefetch=2,
                grid=(tile // step,),
                in_specs=[strip, whole(1, tile)] + [whole(rows, nb)] * n_rounds,
                out_specs=[whole(rows, nb)] * n_rounds + [whole(nb, nb), whole(2, tile, nb)],
                scratch_shapes=[
                    pltpu.VMEM((2, tile, 2 * nb), BF16),
                    pltpu.VMEM((2, nb, tile), BF16),
                    pltpu.VMEM((2, nb, tile), BF16),
                    pltpu.VMEM((2, tile, nb), F32),
                    pltpu.VMEM((2, nb, tile), F32),
                ],
            ),
            compiler_params=pltpu.CompilerParams(dimension_semantics=("arbitrary",)),
            name="z_block",
        )(slots, flags, matrix, far_diag, *v_in)
        z_parts, g_part, v_pair = outs[:n_rounds], outs[n_rounds], outs[n_rounds + 1]

        z_here = [lax.ppermute(part, AXES, perm) for part, perm in zip(z_parts, up)]
        gram = all_sum(g_part)
        z_home = functools.reduce(lambda a, b: a + b, z_here)
        z_in = [lax.ppermute(z_home, AXES, perm) for perm in down]

        hi, lo, far_own = pl.pallas_call(
            functools.partial(w_kernel, n_rounds),
            out_shape=[
                jax.ShapeDtypeStruct((2, tile, 2 * nb), BF16),
                jax.ShapeDtypeStruct((2, tile, 2 * nb), BF16),
                jax.ShapeDtypeStruct((1, tile), F32),
            ],
            grid_spec=pltpu.PrefetchScalarGridSpec(
                num_scalar_prefetch=2,
                grid=(1,),
                in_specs=[whole(2, tile, nb), whole(nb, nb), whole(nb, nb), whole(1, tile)]
                + [whole(rows, nb)] * n_rounds,
                out_specs=[whole(2, tile, 2 * nb), whole(2, tile, 2 * nb), whole(1, tile)],
                scratch_shapes=[pltpu.VMEM((2, tile, nb), F32)],
            ),
            name="w_block",
        )(slots, flags, v_pair, gram, factors, far_diag, *z_in)
        far_sent = lax.ppermute(far_own, AXES, far_perm)

        updated = pl.pallas_call(
            functools.partial(u_kernel, step),
            out_shape=jax.ShapeDtypeStruct((tile, tile), F32),
            grid_spec=pltpu.PrefetchScalarGridSpec(
                num_scalar_prefetch=2,
                grid=(tile // step,),
                in_specs=[strip, whole(2, tile, 2 * nb), whole(2, tile, 2 * nb)],
                out_specs=strip,
                scratch_shapes=[
                    pltpu.VMEM((2, tile, 2 * nb), BF16),
                    pltpu.VMEM((2, tile, 2 * nb), BF16),
                ],
            ),
            compiler_params=pltpu.CompilerParams(dimension_semantics=("arbitrary",)),
            cost_estimate=pl.CostEstimate(
                flops=12 * tile * tile * nb, bytes_accessed=8 * tile * tile, transcendentals=0
            ),
            name="u_block",
        )(slots, flags, matrix, hi, lo)
        far_updated = jnp.where(col_at < row_at, far_sent, far_own)
        return updated, far_updated

    in_specs = (P("row", "col"), P("row", None), P(AXES, None), P())
    out_specs = (P("row", "col"), P("row", None))
    return jax.shard_map(body, mesh=mesh, in_specs=in_specs, out_specs=out_specs, check_vma=False)
```

```python
import functools
import math
import random

import jax
import jax.numpy as jnp
import numpy as np
from jax import lax
from jax.experimental import pallas as pl
from jax.experimental.pallas import tpu as pltpu
from jax.sharding import PartitionSpec as P

AXES = ("row", "col")
F32 = jnp.float32
BF16 = jnp.bfloat16


def tile_pair(grid, h, k):
    if k < h:
        return h, k
    if k == h:
        return h, grid - 1 - h
    return grid - 1 - h, k - h - 1


def place_of(mesh):
    half, grid = mesh.shape["row"], mesh.shape["col"]
    flat = list(mesh.devices.flat)
    spots = [tuple(int(c) for c in getattr(d, "coords", ())) for d in flat]
    if any(len(spot) != 3 for spot in spots):
        spots = [(d // grid // 2, d % grid % 2, d % grid // 2) for d in range(half * grid)]
    low = [min(spot[a] for spot in spots) for a in range(3)]
    spots = [tuple(spot[a] - low[a] for a in range(3)) for spot in spots]
    sizes = [max(spot[a] for spot in spots) + 1 for a in range(3)]
    wraps = [all(size % 4 == 0 for size in sizes)] * 3
    return spots, sizes, wraps


def make_routes(spots, sizes, wraps):
    links = {}
    routes = {}

    def route(src, dst):
        at, end = list(spots[src]), spots[dst]
        path = []
        for axis in (2, 0, 1):
            gap = end[axis] - at[axis]
            size = sizes[axis]
            if wraps[axis] and abs(gap) * 2 > size:
                gap -= size if gap > 0 else -size
            way = 1 if gap > 0 else -1
            for _ in range(abs(gap)):
                path.append(links.setdefault((tuple(at), axis, way), len(links)))
                at[axis] = (at[axis] + way) % size
        return path

    for src in range(len(spots)):
        for dst in range(len(spots)):
            routes[src, dst] = route(src, dst)
    return routes, len(links)


def pick_homes(members, pieces, routes, n_links, steps):
    count = len(members) * pieces
    load = np.zeros((len(members), count, 2 * n_links))
    for tile, group in enumerate(members):
        for home in range(count):
            for member in group:
                np.add.at(load[tile, home], routes[home, member], 1.0)
                np.add.at(load[tile, home], [n_links + l for l in routes[member, home]], 1.0)
    rng = random.Random(5)
    tile_of = [d // pieces for d in range(count)]
    total = sum(load[tile_of[d], d] for d in range(count))

    def score(value):
        return float((value**12).sum() ** (1 / 12) + 0.01 * value.sum() / n_links)

    now = best = score(total)
    kept = list(tile_of)
    heat = now * 0.03
    for _ in range(steps):
        a, b = rng.sample(range(count), 2)
        if tile_of[a] == tile_of[b]:
            continue
        tried = total + load[tile_of[b], a] + load[tile_of[a], b] - load[tile_of[a], a] - load[tile_of[b], b]
        value = score(tried)
        if value < now or rng.random() < math.exp((now - value) / heat):
            now, total = value, tried
            tile_of[a], tile_of[b] = tile_of[b], tile_of[a]
            if now < best:
                best, kept = now, list(tile_of)
        heat *= 0.9998
    home_of = {}
    for tile in range(len(members)):
        spots = [device for device in range(count) if kept[device] == tile]
        first = tile * pieces

        def far(order):
            return sum(len(routes[first + i, device]) ** 3 for i, device in enumerate(order))

        for _ in range(pieces * pieces):
            for i in range(pieces):
                for j in range(i):
                    tried = list(spots)
                    tried[i], tried[j] = spots[j], spots[i]
                    if far(tried) < far(spots):
                        spots = tried
        for i, device in enumerate(spots):
            home_of[first + i] = device
    return home_of


def color_flows(flows, count, hops):
    left = list(flows)
    rounds = []
    for _ in range(len(flows) // count):
        for limit in sorted({hops[f[0], f[1]] for f in left}):
            out_of = [[] for _ in range(count)]
            for index, flow in enumerate(left):
                if hops[flow[0], flow[1]] <= limit:
                    out_of[flow[0]].append(index)
            match = [-1] * count

            def augment(home, seen):
                for index in out_of[home]:
                    member = left[index][1]
                    if member in seen:
                        continue
                    seen.add(member)
                    if match[member] < 0 or augment(left[match[member]][0], seen):
                        match[member] = index
                        return True
                return False

            if all(augment(home, set()) for home in range(count)):
                break
        rounds.append([left[index] for index in match])
        used = set(match)
        left = [flow for index, flow in enumerate(left) if index not in used]
    return rounds


def split(value):
    high = value.astype(BF16)
    return high, (value - high.astype(F32)).astype(BF16)


def dot(left, right):
    return jnp.dot(left, right, preferred_element_type=F32)


def dot_nt(left, right):
    return lax.dot_general(left, right, (((1,), (1,)), ((), ())), preferred_element_type=F32)


def dot3(left, right):
    lh, ll = split(left)
    rh, rl = split(right)
    return dot(lh, rh) + (dot(lh, rl) + dot(ll, rh))


def z_kernel(n_rounds, step, slots, flags, a_ref, d_ref, *refs):
    v_in = refs[:n_rounds]
    z_out = refs[n_rounds:2 * n_rounds]
    g_out, v_out = refs[2 * n_rounds:2 * n_rounds + 2]
    vcat, vt_hi, vt_lo, x_acc, zt_acc = refs[2 * n_rounds + 2:]
    tile = a_ref.shape[1]
    nb = v_in[0].shape[1]
    rows = v_in[0].shape[0]
    count = tile // step
    p = pl.program_id(0)
    diag = flags[0] == 1

    @pl.when(p == 0)
    def _():
        per = tile // rows
        for r in range(n_rounds):
            slot = slots[r]
            role = slot // per
            at = pl.multiple_of((slot % per) * rows, rows)
            v_out[role, pl.ds(at, rows), :] = v_in[r][...]
        for role in range(2):
            for b in range(count):
                cut = slice(b * step, (b + 1) * step)
                v = v_out[role, cut, :]
                vh, vl = split(v)
                vcat[role, cut, 0:nb] = vh
                vcat[role, cut, nb:2 * nb] = vl
                vth, vtl = split(v.T)
                vt_hi[role, :, cut] = vth
                vt_lo[role, :, cut] = vtl
        x_acc[...] = jnp.zeros_like(x_acc)
        zt_acc[...] = jnp.zeros_like(zt_acc)

    p_at = pl.multiple_of(p * step, step)

    def row_part(block, r_role, x_role, q):
        bh, bl = split(block)
        rhs = vcat[r_role, q * step:(q + 1) * step, :]
        both = dot(bh, rhs)
        x_acc[x_role, pl.ds(p_at, step), :] += both[:, :nb] + (both[:, nb:] + dot(bl, rhs[:, :nb]))
        return bh, bl

    def col_part(bh, bl, s_role, y_role, q):
        vth = vt_hi[s_role, :, pl.ds(p_at, step)]
        vtl = vt_lo[s_role, :, pl.ds(p_at, step)]
        zt_acc[y_role, :, q * step:(q + 1) * step] += dot(vth, bh) + (dot(vtl, bh) + dot(vth, bl))

    for q in range(count):
        block = a_ref[:, q * step:(q + 1) * step]

        @pl.when(p != q)
        def _():
            side = jnp.where(q < p, 0, 1)
            bh, bl = row_part(block, jnp.where(diag, side, 1), jnp.where(diag, side, 0), q)
            col_part(bh, bl, jnp.where(diag, side, 0), jnp.where(diag, side, 1), q)

        @pl.when((p == q) & jnp.logical_not(diag))
        def _():
            bh, bl = row_part(block, 1, 0, q)
            col_part(bh, bl, 0, 1, q)

        @pl.when((p == q) & diag)
        def _():
            at_row = lax.broadcasted_iota(jnp.int32, (step, step), 0)
            at_col = lax.broadcasted_iota(jnp.int32, (step, step), 1)
            flip = block.T
            first = jnp.where(at_row >= at_col, block, flip)
            far = d_ref[0:1, q * step:(q + 1) * step]
            second = jnp.where(at_row < at_col, block, jnp.where(at_row > at_col, flip, far))
            row_part(first, 0, 0, q)
            row_part(second, 1, 1, q)

    @pl.when(p == count - 1)
    def _():
        for role in range(2):
            x_acc[role] += zt_acc[role].T
        gram = jnp.zeros((nb, nb), F32)
        for role in range(2):
            zh, zl = split(x_acc[role])
            gram += dot(vt_hi[role], zh) + (dot(vt_lo[role], zh) + dot(vt_hi[role], zl))
        g_out[...] = gram
        per = tile // rows
        for r in range(n_rounds):
            slot = slots[r]
            z_out[r][...] = x_acc[slot // per, pl.ds(pl.multiple_of((slot % per) * rows, rows), rows), :]


def w_kernel(n_rounds, slots, flags, v_ref, g_ref, t_ref, d_ref, *refs):
    z_in = refs[:n_rounds]
    hi_out, lo_out, far_out = refs[n_rounds:n_rounds + 3]
    w_acc = refs[n_rounds + 3]
    rows, nb = z_in[0].shape
    tile = v_ref.shape[1]
    per = tile // rows
    factors = t_ref[...]
    middle = dot3(dot3(factors.T, g_ref[...]), factors)
    half_mid = -0.5 * middle
    for r in range(n_rounds):
        slot = slots[r]
        role = slot // per
        at = pl.multiple_of((slot % per) * rows, rows)
        v = v_ref[role, pl.ds(at, rows), :]
        w = dot3(z_in[r][...], factors) + dot3(v, half_mid)
        vh, vl = split(v)
        wh, wl = split(w)
        w_acc[role, pl.ds(at, rows), :] = w
        hi_out[role, pl.ds(at, rows), 0:nb] = vh
        hi_out[role, pl.ds(at, rows), nb:2 * nb] = wh
        lo_out[role, pl.ds(at, rows), 0:nb] = vl
        lo_out[role, pl.ds(at, rows), nb:2 * nb] = wl
    far_role = flags[1]
    prod = v_ref[far_role] * w_acc[far_role]
    total = jnp.sum(prod.T, axis=0, keepdims=True)
    far_out[...] = d_ref[...] - 2.0 * total


def u_kernel(step, slots, flags, a_ref, hi_ref, lo_ref, out_ref, qh_ref, ql_ref):
    tile = a_ref.shape[1]
    nb = hi_ref.shape[2] // 2
    count = tile // step
    p = pl.program_id(0)
    diag = flags[0] == 1
    p_at = pl.multiple_of(p * step, step)

    @pl.when(p == 0)
    def _():
        for role in range(2):
            qh_ref[role, :, 0:nb] = hi_ref[role, :, nb:2 * nb]
            qh_ref[role, :, nb:2 * nb] = hi_ref[role, :, 0:nb]
            ql_ref[role, :, 0:nb] = lo_ref[role, :, nb:2 * nb]
            ql_ref[role, :, nb:2 * nb] = lo_ref[role, :, 0:nb]

    def change(left, right, q):
        cut = slice(q * step, (q + 1) * step)
        ph = hi_ref[left, pl.ds(p_at, step), :]
        plo = lo_ref[left, pl.ds(p_at, step), :]
        qh = qh_ref[right, cut, :]
        ql = ql_ref[right, cut, :]
        return dot_nt(ph, qh) + (dot_nt(ph, ql) + dot_nt(plo, qh))

    for q in range(count):
        cut = slice(q * step, (q + 1) * step)

        @pl.when((p != q) | jnp.logical_not(diag))
        def _():
            side = jnp.where(q < p, 0, 1)
            out_ref[:, cut] = a_ref[:, cut] - change(
                jnp.where(diag, side, 0), jnp.where(diag, side, 1), q
            )

        @pl.when((p == q) & diag)
        def _():
            at_row = lax.broadcasted_iota(jnp.int32, (step, step), 0)
            at_col = lax.broadcasted_iota(jnp.int32, (step, step), 1)
            out_ref[:, cut] = a_ref[:, cut] - jnp.where(
                at_row >= at_col, change(0, 0, q), change(1, 1, q)
            )


def solution(mesh):
    half, grid = mesh.shape["row"], mesh.shape["col"]
    count = half * grid
    pieces = half
    spots, sizes, wraps = place_of(mesh)
    routes, n_links = make_routes(spots, sizes, wraps)
    hops = {pair: len(path) for pair, path in routes.items()}
    pairs = [tile_pair(grid, *divmod(d, grid)) for d in range(count)]
    members = [[d for d in range(count) if tile in pairs[d]] for tile in range(grid)]
    home_of = pick_homes(members, pieces, routes, n_links, 12000)
    flows = [
        (home_of[tile * pieces + piece], d, role * pieces + piece)
        for d in range(count)
        for role, tile in enumerate(pairs[d])
        for piece in range(pieces)
    ]
    rounds = color_flows(flows, count, hops)
    n_rounds = len(rounds)
    slot_table = np.zeros((count, n_rounds), np.int32)
    for r, part in enumerate(rounds):
        for _, member, slot in part:
            slot_table[member, r] = slot
    down = [[(home, member) for home, member, _ in part] for part in rounds]
    up = [[(member, home) for home, member, _ in part] for part in rounds]
    settle = [(d, home_of[d]) for d in range(count)]
    far_perm = [
        (h * grid + k + h, h * grid + k) for h in range(half) for k in range(h)
    ]

    def all_sum(value):
        gap = 1
        while gap < count:
            perm = [(d, d ^ gap) for d in range(count)]
            value = value + lax.ppermute(value, AXES, perm)
            gap *= 2
        return value

    def body(matrix, far_diag, vectors, factors):
        tile = matrix.shape[0]
        rows, nb = vectors.shape
        step = tile // 3 if tile % 384 == 0 else tile
        row_at = lax.axis_index("row")
        col_at = lax.axis_index("col")
        me = row_at * grid + col_at
        slots = lax.dynamic_slice_in_dim(jnp.asarray(slot_table), me, 1, 0)[0]
        flags = jnp.stack(
            [(col_at == row_at).astype(jnp.int32), (col_at == row_at).astype(jnp.int32)]
        )
        v_home = lax.ppermute(vectors, AXES, settle)
        v_in = [lax.ppermute(v_home, AXES, perm) for perm in down]
        whole = lambda *shape: pl.BlockSpec(shape, lambda p, *_: (0,) * len(shape))
        strip = pl.BlockSpec((step, tile), lambda p, *_: (p, 0))
        piece = jax.ShapeDtypeStruct((rows, nb), F32)

        outs = pl.pallas_call(
            functools.partial(z_kernel, n_rounds, step),
            out_shape=[piece] * n_rounds
            + [jax.ShapeDtypeStruct((nb, nb), F32), jax.ShapeDtypeStruct((2, tile, nb), F32)],
            grid_spec=pltpu.PrefetchScalarGridSpec(
                num_scalar_prefetch=2,
                grid=(tile // step,),
                in_specs=[strip, whole(1, tile)] + [whole(rows, nb)] * n_rounds,
                out_specs=[whole(rows, nb)] * n_rounds + [whole(nb, nb), whole(2, tile, nb)],
                scratch_shapes=[
                    pltpu.VMEM((2, tile, 2 * nb), BF16),
                    pltpu.VMEM((2, nb, tile), BF16),
                    pltpu.VMEM((2, nb, tile), BF16),
                    pltpu.VMEM((2, tile, nb), F32),
                    pltpu.VMEM((2, nb, tile), F32),
                ],
            ),
            compiler_params=pltpu.CompilerParams(dimension_semantics=("arbitrary",)),
            name="z_block",
        )(slots, flags, matrix, far_diag, *v_in)
        z_parts, g_part, v_pair = outs[:n_rounds], outs[n_rounds], outs[n_rounds + 1]

        z_here = [lax.ppermute(part, AXES, perm) for part, perm in zip(z_parts, up)]
        gram = all_sum(g_part)
        z_home = functools.reduce(lambda a, b: a + b, z_here)
        z_in = [lax.ppermute(z_home, AXES, perm) for perm in down]

        hi, lo, far_own = pl.pallas_call(
            functools.partial(w_kernel, n_rounds),
            out_shape=[
                jax.ShapeDtypeStruct((2, tile, 2 * nb), BF16),
                jax.ShapeDtypeStruct((2, tile, 2 * nb), BF16),
                jax.ShapeDtypeStruct((1, tile), F32),
            ],
            grid_spec=pltpu.PrefetchScalarGridSpec(
                num_scalar_prefetch=2,
                grid=(1,),
                in_specs=[whole(2, tile, nb), whole(nb, nb), whole(nb, nb), whole(1, tile)]
                + [whole(rows, nb)] * n_rounds,
                out_specs=[whole(2, tile, 2 * nb), whole(2, tile, 2 * nb), whole(1, tile)],
                scratch_shapes=[pltpu.VMEM((2, tile, nb), F32)],
            ),
            name="w_block",
        )(slots, flags, v_pair, gram, factors, far_diag, *z_in)
        far_sent = lax.ppermute(far_own, AXES, far_perm)

        updated = pl.pallas_call(
            functools.partial(u_kernel, step),
            out_shape=jax.ShapeDtypeStruct((tile, tile), F32),
            grid_spec=pltpu.PrefetchScalarGridSpec(
                num_scalar_prefetch=2,
                grid=(tile // step,),
                in_specs=[strip, whole(2, tile, 2 * nb), whole(2, tile, 2 * nb)],
                out_specs=strip,
                scratch_shapes=[
                    pltpu.VMEM((2, tile, 2 * nb), BF16),
                    pltpu.VMEM((2, tile, 2 * nb), BF16),
                ],
            ),
            compiler_params=pltpu.CompilerParams(dimension_semantics=("arbitrary",)),
            cost_estimate=pl.CostEstimate(
                flops=12 * tile * tile * nb, bytes_accessed=8 * tile * tile, transcendentals=0
            ),
            name="u_block",
        )(slots, flags, matrix, hi, lo)
        far_updated = jnp.where(col_at < row_at, far_sent, far_own)
        return updated, far_updated

    in_specs = (P("row", "col"), P("row", None), P(AXES, None), P())
    out_specs = (P("row", "col"), P("row", None))
    return jax.shard_map(body, mesh=mesh, in_specs=in_specs, out_specs=out_specs, check_vma=False)
```

```python
import functools
import math
import random

import jax
import jax.numpy as jnp
import numpy as np
from jax import lax
from jax.experimental import pallas as pl
from jax.experimental.pallas import tpu as pltpu
from jax.sharding import PartitionSpec as P


AXES = ("row", "col")
F32 = jnp.float32
BF16 = jnp.bfloat16


def tile_pair(grid, h, k):
    if k < h:
        return h, k
    if k == h:
        return h, grid - 1 - h
    return grid - 1 - h, k - h - 1


def place_of(mesh):
    half, grid = mesh.shape["row"], mesh.shape["col"]
    flat = list(mesh.devices.flat)
    spots = [tuple(int(c) for c in getattr(d, "coords", ())) for d in flat]
    if any(len(spot) != 3 for spot in spots):
        spots = [(d // grid // 2, d % grid % 2, d % grid // 2) for d in range(half * grid)]
    low = [min(spot[a] for spot in spots) for a in range(3)]
    spots = [tuple(spot[a] - low[a] for a in range(3)) for spot in spots]
    sizes = [max(spot[a] for spot in spots) + 1 for a in range(3)]
    wraps = [all(size % 4 == 0 for size in sizes)] * 3
    return spots, sizes, wraps


def make_routes(spots, sizes, wraps):
    links = {}
    routes = {}

    def route(src, dst):
        at, end = list(spots[src]), spots[dst]
        path = []
        for axis in (2, 0, 1):
            gap = end[axis] - at[axis]
            size = sizes[axis]
            if wraps[axis] and abs(gap) * 2 > size:
                gap -= size if gap > 0 else -size
            way = 1 if gap > 0 else -1
            for _ in range(abs(gap)):
                path.append(links.setdefault((tuple(at), axis, way), len(links)))
                at[axis] = (at[axis] + way) % size
        return path

    for src in range(len(spots)):
        for dst in range(len(spots)):
            routes[src, dst] = route(src, dst)
    return routes, len(links)


def pick_homes(parts, steps):
    n_units, n_chips = parts[0].shape[:2]
    rng = random.Random(5)

    def score(totals):
        return sum(float((t**12).sum() ** (1 / 12)) + 0.2 * float(t.mean()) for t in totals)

    best, kept = math.inf, None
    for _ in range(3):
        chip_of = list(range(n_chips))
        totals = [sum(part[u, chip_of[u]] for u in range(n_units)) for part in parts]
        now = score(totals)
        heat = now * 0.03
        for _ in range(steps):
            a, b = rng.sample(range(n_units), 2)
            x, y = chip_of[a], chip_of[b]
            tried = [t + p[a, y] + p[b, x] - p[a, x] - p[b, y] for t, p in zip(totals, parts)]
            value = score(tried)
            if value < now or rng.random() < math.exp((now - value) / heat):
                now, totals = value, tried
                chip_of[a], chip_of[b] = y, x
                if now < best:
                    best, kept = now, list(chip_of)
            heat *= 0.9995
    return kept


def load_of(routes, n_links, pairs):
    load = np.zeros(n_links)
    for pair in pairs:
        np.add.at(load, routes[pair], 1.0)
    return load


def color_flows(flows, chips, count, hops):
    left = list(flows)
    rounds = []
    for _ in range(len(flows) // count):
        for limit in sorted({hops[chips[f[0]][0], f[1]] for f in left}):
            into = [[] for _ in range(count)]
            for index, (chip, member, _) in enumerate(left):
                if hops[chips[chip][0], member] <= limit:
                    into[member].append(index)
            match = {}

            def augment(member, seen):
                for index in into[member]:
                    for core in chips[left[index][0]]:
                        if core in seen:
                            continue
                        seen.add(core)
                        if core not in match or augment(left[match[core]][1], seen):
                            match[core] = index
                            return True
                return False

            if all(augment(member, set()) for member in range(count)):
                break
        for first, second in chips:
            if left[match[first]][1] == second or left[match[second]][1] == first:
                match[first], match[second] = match[second], match[first]
        rounds.append([(core, left[match[core]][1], left[match[core]][2]) for core in range(count)])
        used = set(match.values())
        left = [flow for index, flow in enumerate(left) if index not in used]
    return rounds


def split(value):
    high = value.astype(BF16)
    return high, (value - high.astype(F32)).astype(BF16)


def dot(left, right):
    return jnp.dot(left, right, preferred_element_type=F32)


def dot_nt(left, right):
    return lax.dot_general(left, right, (((1,), (1,)), ((), ())), preferred_element_type=F32)


def dot3(left, right):
    lh, ll = split(left)
    rh, rl = split(right)
    return dot(lh, rh) + (dot(lh, rl) + dot(ll, rh))


def split_kernel(step, a_hbm, high_ref, low_ref, stage, sems):
    count = stage.shape[0] // step

    def copy_in(i):
        here = slice(i * step, (i + 1) * step)
        return pltpu.make_async_copy(a_hbm.at[here, :], stage.at[here, :], sems.at[i])

    for i in range(count):
        copy_in(i).start()
    for i in range(count):
        here = slice(i * step, (i + 1) * step)
        copy_in(i).wait()
        high_ref[here, :], low_ref[here, :] = split(stage[here, :])


def load_kernel(step, a_hbm, a_ref, sems):
    count = a_ref.shape[0] // step

    def copy_in(i):
        here = slice(i * step, (i + 1) * step)
        return pltpu.make_async_copy(a_hbm.at[here, :], a_ref.at[here, :], sems.at[i])

    for i in range(count):
        copy_in(i).start()
    for i in range(count):
        copy_in(i).wait()


def z_kernel(n_rounds, step, v_slots, slots, flags, high_ref, low_ref, d_ref, *refs):
    v_in = refs[:n_rounds]
    z_out = refs[n_rounds:2 * n_rounds]
    g_out = refs[2 * n_rounds]
    v_all, vcat, vt, x_acc, zt_acc = refs[2 * n_rounds + 1:]
    tile = high_ref.shape[1]
    unit, nb = v_in[0].shape
    rows = unit // 2
    count = tile // step
    diag = flags[0] == 1
    per = tile // rows
    for r in range(n_rounds):
        for half in range(2):
            slot = v_slots[2 * r + half]
            at = pl.multiple_of((slot % per) * rows, rows)
            v_all[slot // per, pl.ds(at, rows), :] = v_in[r][half * rows:(half + 1) * rows, :]
    for role in range(2):
        for b in range(count):
            cut = slice(b * step, (b + 1) * step)
            v = v_all[role, cut, :]
            vh, vl = split(v)
            vcat[role, cut, 0:nb] = vh
            vcat[role, cut, nb:2 * nb] = vl
            vth, vtl = split(v.T)
            vt[role, 0:nb, cut] = vth
            vt[role, nb:2 * nb, cut] = vtl
    zt_acc[...] = jnp.zeros_like(zt_acc)

    def row_part(bh, bl, role, cut):
        rhs = vcat[role, cut, :]
        both = dot(bh, rhs)
        return both[:, :nb] + (both[:, nb:] + dot(bl, rhs[:, :nb]))

    def col_part(bh, bl, role, here, acc, cut):
        left = vt[role, :, here]
        zt_acc[acc, :, cut] += dot(left, bh)
        zt_acc[acc, 0:nb, cut] += dot(left[:nb], bl)

    every = slice(0, tile)

    @pl.when(jnp.logical_not(diag))
    def _():
        for i in range(count):
            here = slice(i * step, (i + 1) * step)
            bh, bl = high_ref[here, :], low_ref[here, :]
            x_acc[0, here, :] = row_part(bh, bl, 1, every)
            col_part(bh, bl, 0, here, 1, every)
        x_acc[1] = (zt_acc[1, 0:nb] + zt_acc[1, nb:2 * nb]).T

    @pl.when(diag)
    def _():
        at_row = lax.broadcasted_iota(jnp.int32, (step, step), 0)
        at_col = lax.broadcasted_iota(jnp.int32, (step, step), 1)
        for i in range(count):
            low, here, high = slice(0, i * step), slice(i * step, (i + 1) * step), slice((i + 1) * step, tile)
            block = high_ref[here, here].astype(F32) + low_ref[here, here].astype(F32)
            flip = block.T
            first = jnp.where(at_row >= at_col, block, flip)
            second = jnp.where(at_row < at_col, block, jnp.where(at_row > at_col, flip, d_ref[0:1, here]))
            for role, mid, cut in ((0, first, low), (1, second, high)):
                total = row_part(*split(mid), role, here)
                if cut.stop > cut.start:
                    bh, bl = high_ref[here, cut], low_ref[here, cut]
                    total += row_part(bh, bl, role, cut)
                    col_part(bh, bl, role, here, role, cut)
                x_acc[role, here, :] = total
        for role in range(2):
            x_acc[role] += (zt_acc[role, 0:nb] + zt_acc[role, nb:2 * nb]).T

    gram = jnp.zeros((2 * nb, nb), F32)
    low_part = jnp.zeros((nb, nb), F32)
    for role in range(2):
        zh, zl = split(x_acc[role])
        gram += dot(vt[role], zh)
        low_part += dot(vt[role, 0:nb], zl)
    g_out[...] = gram[:nb] + (gram[nb:] + low_part)
    per = tile // unit
    for r in range(n_rounds):
        slot = slots[r]
        z_out[r][...] = x_acc[slot // per, pl.ds(pl.multiple_of((slot % per) * unit, unit), unit), :]


def w_kernel(n_rounds, v_slots, slots, flags, g_ref, t_ref, d_ref, *refs):
    v_in = refs[:n_rounds]
    z_in = refs[n_rounds:2 * n_rounds]
    hi_out, lo_out, far_out = refs[2 * n_rounds:2 * n_rounds + 3]
    v_all, w_all = refs[2 * n_rounds + 3:]
    unit, nb = z_in[0].shape
    rows = unit // 2
    tile = v_all.shape[1]
    per = tile // rows
    for r in range(n_rounds):
        for half in range(2):
            slot = v_slots[2 * r + half]
            at = pl.multiple_of((slot % per) * rows, rows)
            v_all[slot // per, pl.ds(at, rows), :] = v_in[r][half * rows:(half + 1) * rows, :]
    factors = t_ref[...]
    fh, fl = split(factors)
    mh, ml = split(-0.5 * dot3(dot3(factors.T, g_ref[...]), factors))
    top = jnp.concatenate([jnp.concatenate([fh, fl], 1), jnp.concatenate([mh, ml], 1)], 0)
    low = jnp.concatenate([fh, mh], 0)
    per = tile // unit
    for r in range(n_rounds):
        slot = slots[r]
        role = slot // per
        at = pl.multiple_of((slot % per) * unit, unit)
        v = v_all[role, pl.ds(at, unit), :]
        vh, vl = split(v)
        zh, zl = split(z_in[r][...])
        both = dot(jnp.concatenate([zh, vh], 1), top)
        w = both[:, :nb] + (both[:, nb:] + dot(jnp.concatenate([zl, vl], 1), low))
        wh, wl = split(w)
        w_all[role, pl.ds(at, unit), :] = w
        hi_out[role, pl.ds(at, unit), 0:nb] = vh
        hi_out[role, pl.ds(at, unit), nb:2 * nb] = wh
        lo_out[role, pl.ds(at, unit), 0:nb] = vl
        lo_out[role, pl.ds(at, unit), nb:2 * nb] = wl
    far_role = flags[1]
    prod = v_all[far_role] * w_all[far_role]
    ones = jnp.ones((8, nb), BF16)
    ph, rest = split(prod)
    total = dot_nt(ones, ph) + dot_nt(ones, rest)
    far_out[...] = d_ref[...] - 2.0 * total[0:1, :]


def u_kernel(step, flags, a_ref, hi_ref, lo_ref, out_ref, new, sems):
    tile = a_ref.shape[1]
    nb = hi_ref.shape[2] // 2
    count = tile // step
    diag = flags[0] == 1

    def change(left, right, here, cut):
        lh = hi_ref[left, here, :]
        ll = lo_ref[left, here, :]
        lh = jnp.concatenate([lh[:, nb:], lh[:, :nb]], 1)
        ll = jnp.concatenate([ll[:, nb:], ll[:, :nb]], 1)
        qh = hi_ref[right, cut, :]
        ql = lo_ref[right, cut, :]
        return dot_nt(lh, qh) + dot_nt(lh, ql) + dot_nt(ll, qh)

    def copy_out(i):
        here = slice(i * step, (i + 1) * step)
        return pltpu.make_async_copy(new.at[here, :], out_ref.at[here, :], sems.at[i])

    for i in range(count):
        low, here, high = slice(0, i * step), slice(i * step, (i + 1) * step), slice((i + 1) * step, tile)

        @pl.when(jnp.logical_not(diag))
        def _():
            new[here, :] = a_ref[here, :] - change(0, 1, here, slice(0, tile))

        @pl.when(diag)
        def _():
            at_row = lax.broadcasted_iota(jnp.int32, (step, step), 0)
            at_col = lax.broadcasted_iota(jnp.int32, (step, step), 1)
            mid = jnp.where(at_row >= at_col, change(0, 0, here, here), change(1, 1, here, here))
            new[here, here] = a_ref[here, here] - mid
            for role, cut in ((0, low), (1, high)):
                if cut.stop > cut.start:
                    new[here, cut] = a_ref[here, cut] - change(role, role, here, cut)

        copy_out(i).start()
    for i in range(count):
        copy_out(i).wait()


def solution(mesh):
    half, grid = mesh.shape["row"], mesh.shape["col"]
    count = half * grid
    units = half // 2
    spots, sizes, wraps = place_of(mesh)
    routes, n_links = make_routes(spots, sizes, wraps)
    hops = {pair: len(path) for pair, path in routes.items()}
    chips = [[d for d in range(count) if spots[d] == spot] for spot in sorted(set(spots))]
    pairs = [tile_pair(grid, *divmod(d, grid)) for d in range(count)]
    members = [[d for d in range(count) if tile in pairs[d]] for tile in range(grid)]
    n_units = grid * units
    chip_load = lambda ends: np.array(
        [[load_of(routes, n_links, ends(u, cores)) for cores in chips] for u in range(n_units)]
    )
    down_load = chip_load(lambda u, cores: [(cores[0], m) for m in members[u // units] for _ in range(2)])
    up_load = chip_load(lambda u, cores: [(m, cores[0]) for m in members[u // units] for _ in range(2)])
    settle_load = chip_load(lambda u, cores: [(2 * u + c, cores[c]) for c in range(2)])
    v_chip = pick_homes([down_load, settle_load], 12000)
    z_chip = pick_homes([down_load, up_load], 12000)

    def make_rounds(chip_of):
        flows = [
            (chip_of[tile * units + unit], d, role * units + unit)
            for d in range(count)
            for role, tile in enumerate(pairs[d])
            for unit in range(units)
        ]
        return color_flows(flows, chips, count, hops)

    v_rounds, z_rounds = make_rounds(v_chip), make_rounds(z_chip)
    n_rounds = len(z_rounds)
    second = {cores[1] for cores in chips}
    slot_table = np.zeros((count, 3 * n_rounds), np.int32)
    for r in range(n_rounds):
        for core, member, slot in v_rounds[r]:
            turn = int(core in second)
            slot_table[member, 2 * r:2 * r + 2] = (2 * slot + turn, 2 * slot + 1 - turn)
        for _, member, slot in z_rounds[r]:
            slot_table[member, 2 * n_rounds + r] = slot
    v_down = [[(core, member) for core, member, _ in part] for part in v_rounds]
    z_down = [[(core, member) for core, member, _ in part] for part in z_rounds]
    up = [[(member, core) for core, member, _ in part] for part in z_rounds]
    settle = [(2 * u + c, chips[v_chip[u]][c]) for u in range(n_units) for c in range(2)]
    swap = [pair for a, b in chips for pair in ((a, b), (b, a))]
    far_perm = [
        (h * grid + k + h, h * grid + k) for h in range(half) for k in range(h)
    ]

    def send(value, perm):
        return lax.ppermute(value, AXES, perm)

    gaps = [2**i for i in range(count.bit_length() - 1)]
    gaps.sort(key=lambda gap: hops[0, gap])

    def all_sum(value):
        for gap in gaps:
            value = value + send(value, [(d, d ^ gap) for d in range(count)])
        return value

    def body(matrix, far_diag, vectors, factors):
        tile = matrix.shape[0]
        rows, nb = vectors.shape
        step = next(n for n in (256, 128, tile) if tile % n == 0)
        row_at = lax.axis_index("row")
        col_at = lax.axis_index("col")
        me = row_at * grid + col_at
        table = lax.dynamic_slice_in_dim(jnp.asarray(slot_table), me, 1, 0)[0]
        v_slots, slots = table[:2 * n_rounds], table[2 * n_rounds:]
        flags = jnp.stack(
            [(col_at == row_at).astype(jnp.int32), (col_at == row_at).astype(jnp.int32)]
        )
        v_first = send(vectors, settle)
        v_home = jnp.concatenate([v_first, send(v_first, swap)], axis=0)
        v_in = [send(v_home, perm) for perm in v_down]
        smem = pl.BlockSpec(memory_space=pltpu.SMEM)
        vmem = pl.BlockSpec(memory_space=pltpu.VMEM)
        unit = 2 * rows
        piece = jax.ShapeDtypeStruct((unit, nb), F32)

        hbm = pl.BlockSpec(memory_space=pltpu.HBM)
        keep = lambda value: pltpu.with_memory_space_constraint(value, pltpu.VMEM)
        cost = pl.CostEstimate(flops=4 * tile * tile, bytes_accessed=8 * tile * tile, transcendentals=0)
        copies = pltpu.SemaphoreType.DMA((tile // step,))
        high, low = pl.pallas_call(
            functools.partial(split_kernel, step),
            out_shape=[pltpu.MemorySpace.VMEM((tile, tile), BF16)] * 2,
            in_specs=[hbm],
            out_specs=[vmem] * 2,
            scratch_shapes=[pltpu.VMEM((tile, tile), F32), copies],
            compiler_params=pltpu.CompilerParams(vmem_limit_bytes=12 * 2**20),
            cost_estimate=cost,
            name="split_block",
        )(matrix)
        block = pl.pallas_call(
            functools.partial(load_kernel, step),
            out_shape=pltpu.MemorySpace.VMEM((tile, tile), F32),
            in_specs=[hbm],
            out_specs=vmem,
            scratch_shapes=[copies],
            compiler_params=pltpu.CompilerParams(vmem_limit_bytes=4 * 2**20),
            cost_estimate=cost,
            name="load_block",
        )(matrix)
        outs = pl.pallas_call(
            functools.partial(z_kernel, n_rounds, step),
            out_shape=[piece] * n_rounds + [jax.ShapeDtypeStruct((nb, nb), F32)],
            in_specs=[smem] * 3 + [vmem] * (3 + n_rounds),
            out_specs=[vmem] * (n_rounds + 1),
            scratch_shapes=[
                pltpu.VMEM((2, tile, nb), F32),
                pltpu.VMEM((2, tile, 2 * nb), BF16),
                pltpu.VMEM((2, 2 * nb, tile), BF16),
                pltpu.VMEM((2, tile, nb), F32),
                pltpu.VMEM((2, 2 * nb, tile), F32),
            ],
            compiler_params=pltpu.CompilerParams(vmem_limit_bytes=20 * 2**20),
            name="z_block",
        )(v_slots, slots, flags, keep(high), keep(low), far_diag, *v_in)
        z_parts, g_part = outs[:n_rounds], outs[n_rounds]

        z_here = [send(z_parts[r], perm) for r, perm in enumerate(up)]
        gram = all_sum(g_part)
        z_sum = functools.reduce(lambda a, b: a + b, z_here)
        z_home = z_sum + send(z_sum, swap)
        z_in = [send(z_home, perm) for perm in z_down]

        hi, lo, far_own = pl.pallas_call(
            functools.partial(w_kernel, n_rounds),
            out_shape=[
                jax.ShapeDtypeStruct((2, tile, 2 * nb), BF16),
                jax.ShapeDtypeStruct((2, tile, 2 * nb), BF16),
                jax.ShapeDtypeStruct((1, tile), F32),
            ],
            in_specs=[smem] * 3 + [vmem] * (3 + 2 * n_rounds),
            out_specs=[vmem] * 3,
            scratch_shapes=[pltpu.VMEM((2, tile, nb), F32), pltpu.VMEM((2, tile, nb), F32)],
            compiler_params=pltpu.CompilerParams(vmem_limit_bytes=16 * 2**20),
            name="w_block",
        )(v_slots, slots, flags, gram, factors, far_diag, *v_in, *z_in)
        far_sent = lax.ppermute(far_own, AXES, far_perm)

        updated = pl.pallas_call(
            functools.partial(u_kernel, step),
            out_shape=jax.ShapeDtypeStruct((tile, tile), F32),
            in_specs=[smem, vmem, vmem, vmem],
            out_specs=pl.BlockSpec(memory_space=pl.ANY),
            scratch_shapes=[pltpu.VMEM((tile, tile), F32), pltpu.SemaphoreType.DMA((tile // step,))],
            compiler_params=pltpu.CompilerParams(vmem_limit_bytes=20 * 2**20),
            cost_estimate=pl.CostEstimate(
                flops=12 * tile * tile * nb, bytes_accessed=8 * tile * tile, transcendentals=0
            ),
            name="u_block",
        )(flags, keep(block), hi, lo)
        far_updated = jnp.where(col_at < row_at, far_sent, far_own)
        return updated, far_updated

    in_specs = (P("row", "col"), P("row", None), P(AXES, None), P())
    out_specs = (P("row", "col"), P("row", None))
    return jax.shard_map(body, mesh=mesh, in_specs=in_specs, out_specs=out_specs, check_vma=False)
```

```python
import functools
import math
import random

import jax
import jax.numpy as jnp
import numpy as np
from jax import lax
from jax.experimental import pallas as pl
from jax.experimental.pallas import tpu as pltpu
from jax.sharding import PartitionSpec as P


AXES = ("row", "col")
V_HOMES, V_ROUNDS, Z_HOMES, Z_ROUNDS = 5, 961, 8, 566
F32 = jnp.float32
BF16 = jnp.bfloat16


def tile_pair(grid, h, k):
    if k < h:
        return h, k
    if k == h:
        return h, grid - 1 - h
    return grid - 1 - h, k - h - 1


def place_of(mesh):
    half, grid = mesh.shape["row"], mesh.shape["col"]
    flat = list(mesh.devices.flat)
    spots = [tuple(int(c) for c in getattr(d, "coords", ())) for d in flat]
    if any(len(spot) != 3 for spot in spots):
        spots = [(d // grid // 2, d % grid % 2, d % grid // 2) for d in range(half * grid)]
    low = [min(spot[a] for spot in spots) for a in range(3)]
    spots = [tuple(spot[a] - low[a] for a in range(3)) for spot in spots]
    sizes = [max(spot[a] for spot in spots) + 1 for a in range(3)]
    wraps = [all(size % 4 == 0 for size in sizes)] * 3
    return spots, sizes, wraps


def make_routes(spots, sizes, wraps):
    links = {}
    routes = {}

    def route(src, dst):
        at, end = list(spots[src]), spots[dst]
        path = []
        for axis in (2, 0, 1):
            gap = end[axis] - at[axis]
            size = sizes[axis]
            if wraps[axis] and abs(gap) * 2 > size:
                gap -= size if gap > 0 else -size
            way = 1 if gap > 0 else -1
            for _ in range(abs(gap)):
                path.append(links.setdefault((tuple(at), axis, way), len(links)))
                at[axis] = (at[axis] + way) % size
        return path

    for src in range(len(spots)):
        for dst in range(len(spots)):
            routes[src, dst] = route(src, dst)
    return routes, len(links)


def pick_homes(parts, steps, seed):
    n_units, n_chips = parts[0].shape[:2]
    rng = random.Random(seed)

    def score(totals):
        return sum(float((t**12).sum() ** (1 / 12)) + 0.2 * float(t.mean()) for t in totals)

    best, kept = math.inf, None
    for _ in range(3):
        chip_of = list(range(n_chips))
        rng.shuffle(chip_of)
        totals = [sum(part[u, chip_of[u]] for u in range(n_units)) for part in parts]
        now = score(totals)
        heat = now * 0.03
        for _ in range(steps):
            a, b = rng.sample(range(n_units), 2)
            x, y = chip_of[a], chip_of[b]
            tried = [t + p[a, y] + p[b, x] - p[a, x] - p[b, y] for t, p in zip(totals, parts)]
            value = score(tried)
            if value < now or rng.random() < math.exp((now - value) / heat):
                now, totals = value, tried
                chip_of[a], chip_of[b] = y, x
                if now < best:
                    best, kept = now, list(chip_of)
            heat *= 0.9995
    return kept


def load_of(routes, n_links, pairs):
    load = np.zeros(n_links)
    for pair in pairs:
        np.add.at(load, routes[pair], 1.0)
    return load


def color_flows(flows, chips, count, hops, seed):
    rng = random.Random(seed)
    left = list(flows)
    rng.shuffle(left)
    rounds = []
    for _ in range(len(flows) // count):
        for limit in sorted({hops[chips[f[0]][0], f[1]] for f in left}):
            into = [[] for _ in range(count)]
            for index, (chip, member, _) in enumerate(left):
                if hops[chips[chip][0], member] <= limit:
                    into[member].append(index)
            match = {}

            def augment(member, seen):
                for index in into[member]:
                    for core in rng.sample(chips[left[index][0]], 2):
                        if core in seen:
                            continue
                        seen.add(core)
                        if core not in match or augment(left[match[core]][1], seen):
                            match[core] = index
                            return True
                return False

            if all(augment(member, set()) for member in range(count)):
                break
        for first, second in chips:
            if left[match[first]][1] == second or left[match[second]][1] == first:
                match[first], match[second] = match[second], match[first]
        rounds.append([(core, left[match[core]][1], left[match[core]][2]) for core in range(count)])
        used = set(match.values())
        left = [flow for index, flow in enumerate(left) if index not in used]
    return rounds


def even_rounds(rounds, chips, routes, n_links, upward, steps, seed):
    rng = random.Random(seed)
    count = len(rounds[0])
    chip_of = {core: chip for chip, cores in enumerate(chips) for core in cores}
    source = [[0] * count for _ in rounds]
    slot_at = [[0] * count for _ in rounds]
    for r, part in enumerate(rounds):
        for core, member, slot in part:
            source[r][member], slot_at[r][member] = chip_of[core], slot
    path = np.zeros((len(chips), count, n_links))
    for chip, cores in enumerate(chips):
        for member in range(count):
            pair = (member, cores[0]) if upward else (cores[0], member)
            np.add.at(path[chip, member], routes[pair], 1.0)
    loads = [sum(path[source[r][m], m] for m in range(count)) for r in range(len(rounds))]
    score = lambda parts: [float((part**8).sum() ** 0.125) for part in parts]
    cost = score(loads)
    heat = 0.05 * max(cost)
    best, kept = sum(cost), [list(s) for s in source]
    kept_slots = [list(s) for s in slot_at]
    for _ in range(steps):
        heat *= 1.0 - 5.0 / steps
        one, two = rng.sample(range(len(rounds)), 2)
        chain = [rng.randrange(count)]
        goal, at = source[two][chain[0]], source[one][chain[0]]
        while at != goal and len(chain) < 12:
            nexts = [m for m in range(count) if source[two][m] == at and m not in chain]
            if not nexts:
                break
            chain.append(rng.choice(nexts))
            at = source[one][chain[-1]]
        if at != goal:
            continue
        shift = sum(path[source[two][m], m] - path[source[one][m], m] for m in chain)
        tried = score([loads[one] + shift, loads[two] - shift])
        gain = cost[one] + cost[two] - sum(tried)
        if gain > 0 or rng.random() < math.exp(gain / heat):
            loads[one], loads[two] = loads[one] + shift, loads[two] - shift
            cost[one], cost[two] = tried
            for m in chain:
                for table in (source, slot_at):
                    table[one][m], table[two][m] = table[two][m], table[one][m]
            if sum(cost) < best - 1e-9:
                best, kept = sum(cost), [list(s) for s in source]
                kept_slots = [list(s) for s in slot_at]
    result = []
    for r in range(len(rounds)):
        taken = {}
        for member in sorted(range(count), key=lambda m: m not in chips[kept[r][m]]):
            cores = [c for c in chips[kept[r][member]] if c not in taken]
            core = member if member in cores else cores[0]
            taken[core] = (core, member, kept_slots[r][member])
        result.append((sum(len(routes[c, m]) for c, m, _ in taken.values()), [taken[c] for c in sorted(taken)]))
    result.sort(key=lambda item: item[0])
    return [part for _, part in result]


def split(value):
    high = value.astype(BF16)
    return high, (value - high.astype(F32)).astype(BF16)


def dot(left, right):
    return jnp.dot(left, right, preferred_element_type=F32)


def dot_nt(left, right):
    return lax.dot_general(left, right, (((1,), (1,)), ((), ())), preferred_element_type=F32)


def dot3(left, right):
    lh, ll = split(left)
    rh, rl = split(right)
    return dot(lh, rh) + (dot(lh, rl) + dot(ll, rh))


def split_kernel(step, a_hbm, high_ref, low_ref, stage, sems):
    count = stage.shape[0] // step

    def copy_in(i):
        here = slice(i * step, (i + 1) * step)
        return pltpu.make_async_copy(a_hbm.at[here, :], stage.at[here, :], sems.at[i])

    for i in range(count):
        copy_in(i).start()
    for i in range(count):
        here = slice(i * step, (i + 1) * step)
        copy_in(i).wait()
        high_ref[here, :], low_ref[here, :] = split(stage[here, :])


def load_kernel(step, a_hbm, a_ref, sems):
    count = a_ref.shape[0] // step

    def copy_in(i):
        here = slice(i * step, (i + 1) * step)
        return pltpu.make_async_copy(a_hbm.at[here, :], a_ref.at[here, :], sems.at[i])

    for i in range(count):
        copy_in(i).start()
    for i in range(count):
        copy_in(i).wait()


def z_kernel(n_rounds, step, v_slots, slots, flags, high_ref, low_ref, d_ref, *refs):
    v_in = refs[:n_rounds]
    z_out = refs[n_rounds:2 * n_rounds]
    g_out = refs[2 * n_rounds]
    v_all, vcat, vt, x_acc, zt_acc = refs[2 * n_rounds + 1:]
    tile = high_ref.shape[1]
    unit, nb = v_in[0].shape
    rows = unit // 2
    count = tile // step
    diag = flags[0] == 1
    per = tile // rows
    for r in range(n_rounds):
        for half in range(2):
            slot = v_slots[2 * r + half]
            at = pl.multiple_of((slot % per) * rows, rows)
            v_all[slot // per, pl.ds(at, rows), :] = v_in[r][half * rows:(half + 1) * rows, :]
    for role in range(2):
        for b in range(count):
            cut = slice(b * step, (b + 1) * step)
            v = v_all[role, cut, :]
            vh, vl = split(v)
            vcat[role, cut, 0:nb] = vh
            vcat[role, cut, nb:2 * nb] = vl
            vth, vtl = split(v.T)
            vt[role, 0:nb, cut] = vth
            vt[role, nb:2 * nb, cut] = vtl
    zt_acc[...] = jnp.zeros_like(zt_acc)

    def row_part(bh, bl, role, cut):
        rhs = vcat[role, cut, :]
        both = dot(bh, rhs)
        return both[:, :nb] + (both[:, nb:] + dot(bl, rhs[:, :nb]))

    def col_part(bh, bl, role, here, acc, cut):
        left = vt[role, :, here]
        zt_acc[acc, :, cut] += dot(left, bh)
        zt_acc[acc, 0:nb, cut] += dot(left[:nb], bl)

    every = slice(0, tile)

    @pl.when(jnp.logical_not(diag))
    def _():
        for i in range(count):
            here = slice(i * step, (i + 1) * step)
            bh, bl = high_ref[here, :], low_ref[here, :]
            x_acc[0, here, :] = row_part(bh, bl, 1, every)
            col_part(bh, bl, 0, here, 1, every)
        x_acc[1] = (zt_acc[1, 0:nb] + zt_acc[1, nb:2 * nb]).T

    @pl.when(diag)
    def _():
        at_row = lax.broadcasted_iota(jnp.int32, (step, step), 0)
        at_col = lax.broadcasted_iota(jnp.int32, (step, step), 1)
        for i in range(count):
            low, here, high = slice(0, i * step), slice(i * step, (i + 1) * step), slice((i + 1) * step, tile)
            block = high_ref[here, here].astype(F32) + low_ref[here, here].astype(F32)
            flip = block.T
            first = jnp.where(at_row >= at_col, block, flip)
            second = jnp.where(at_row < at_col, block, jnp.where(at_row > at_col, flip, d_ref[0:1, here]))
            for role, mid, cut in ((0, first, low), (1, second, high)):
                total = row_part(*split(mid), role, here)
                if cut.stop > cut.start:
                    bh, bl = high_ref[here, cut], low_ref[here, cut]
                    total += row_part(bh, bl, role, cut)
                    col_part(bh, bl, role, here, role, cut)
                x_acc[role, here, :] = total
        for role in range(2):
            x_acc[role] += (zt_acc[role, 0:nb] + zt_acc[role, nb:2 * nb]).T

    gram = jnp.zeros((2 * nb, nb), F32)
    low_part = jnp.zeros((nb, nb), F32)
    for role in range(2):
        zh, zl = split(x_acc[role])
        gram += dot(vt[role], zh)
        low_part += dot(vt[role, 0:nb], zl)
    g_out[...] = gram[:nb] + (gram[nb:] + low_part)
    per = tile // unit
    for r in range(n_rounds):
        slot = slots[r]
        z_out[r][...] = x_acc[slot // per, pl.ds(pl.multiple_of((slot % per) * unit, unit), unit), :]


def w_kernel(n_rounds, v_slots, slots, flags, g_ref, t_ref, d_ref, *refs):
    v_in = refs[:n_rounds]
    z_in = refs[n_rounds:2 * n_rounds]
    hi_out, lo_out, far_out = refs[2 * n_rounds:2 * n_rounds + 3]
    v_all, w_all = refs[2 * n_rounds + 3:]
    unit, nb = z_in[0].shape
    rows = unit // 2
    tile = v_all.shape[1]
    per = tile // rows
    for r in range(n_rounds):
        for half in range(2):
            slot = v_slots[2 * r + half]
            at = pl.multiple_of((slot % per) * rows, rows)
            v_all[slot // per, pl.ds(at, rows), :] = v_in[r][half * rows:(half + 1) * rows, :]
    factors = t_ref[...]
    fh, fl = split(factors)
    mh, ml = split(-0.5 * dot3(dot3(factors.T, g_ref[...]), factors))
    top = jnp.concatenate([jnp.concatenate([fh, fl], 1), jnp.concatenate([mh, ml], 1)], 0)
    low = jnp.concatenate([fh, mh], 0)
    per = tile // unit
    for r in range(n_rounds):
        slot = slots[r]
        role = slot // per
        at = pl.multiple_of((slot % per) * unit, unit)
        v = v_all[role, pl.ds(at, unit), :]
        vh, vl = split(v)
        zh, zl = split(z_in[r][...])
        both = dot(jnp.concatenate([zh, vh], 1), top)
        w = both[:, :nb] + (both[:, nb:] + dot(jnp.concatenate([zl, vl], 1), low))
        wh, wl = split(w)
        w_all[role, pl.ds(at, unit), :] = w
        hi_out[role, pl.ds(at, unit), 0:nb] = vh
        hi_out[role, pl.ds(at, unit), nb:2 * nb] = wh
        lo_out[role, pl.ds(at, unit), 0:nb] = vl
        lo_out[role, pl.ds(at, unit), nb:2 * nb] = wl
    far_role = flags[1]
    prod = v_all[far_role] * w_all[far_role]
    ones = jnp.ones((8, nb), BF16)
    ph, rest = split(prod)
    total = dot_nt(ones, ph) + dot_nt(ones, rest)
    far_out[...] = d_ref[...] - 2.0 * total[0:1, :]


def u_kernel(step, flags, a_ref, hi_ref, lo_ref, out_ref, new, sems):
    tile = a_ref.shape[1]
    nb = hi_ref.shape[2] // 2
    count = tile // step
    diag = flags[0] == 1

    def change(left, right, here, cut):
        lh = hi_ref[left, here, :]
        ll = lo_ref[left, here, :]
        lh = jnp.concatenate([lh[:, nb:], lh[:, :nb]], 1)
        ll = jnp.concatenate([ll[:, nb:], ll[:, :nb]], 1)
        qh = hi_ref[right, cut, :]
        ql = lo_ref[right, cut, :]
        return dot_nt(lh, qh) + dot_nt(lh, ql) + dot_nt(ll, qh)

    def copy_out(i):
        here = slice(i * step, (i + 1) * step)
        return pltpu.make_async_copy(new.at[here, :], out_ref.at[here, :], sems.at[i])

    for i in range(count):
        low, here, high = slice(0, i * step), slice(i * step, (i + 1) * step), slice((i + 1) * step, tile)

        @pl.when(jnp.logical_not(diag))
        def _():
            new[here, :] = a_ref[here, :] - change(0, 1, here, slice(0, tile))

        @pl.when(diag)
        def _():
            at_row = lax.broadcasted_iota(jnp.int32, (step, step), 0)
            at_col = lax.broadcasted_iota(jnp.int32, (step, step), 1)
            mid = jnp.where(at_row >= at_col, change(0, 0, here, here), change(1, 1, here, here))
            new[here, here] = a_ref[here, here] - mid
            for role, cut in ((0, low), (1, high)):
                if cut.stop > cut.start:
                    new[here, cut] = a_ref[here, cut] - change(role, role, here, cut)

        copy_out(i).start()
    for i in range(count):
        copy_out(i).wait()


def solution(mesh):
    half, grid = mesh.shape["row"], mesh.shape["col"]
    count = half * grid
    units = half // 2
    spots, sizes, wraps = place_of(mesh)
    routes, n_links = make_routes(spots, sizes, wraps)
    hops = {pair: len(path) for pair, path in routes.items()}
    chips = [[d for d in range(count) if spots[d] == spot] for spot in sorted(set(spots))]
    pairs = [tile_pair(grid, *divmod(d, grid)) for d in range(count)]
    members = [[d for d in range(count) if tile in pairs[d]] for tile in range(grid)]
    n_units = grid * units
    chip_load = lambda ends: np.array(
        [[load_of(routes, n_links, ends(u, cores)) for cores in chips] for u in range(n_units)]
    )
    down_load = chip_load(lambda u, cores: [(cores[0], m) for m in members[u // units] for _ in range(2)])
    up_load = chip_load(lambda u, cores: [(m, cores[0]) for m in members[u // units] for _ in range(2)])
    settle_load = chip_load(lambda u, cores: [(2 * u + c, cores[c]) for c in range(2)])
    v_chip = pick_homes([down_load, settle_load], 12000, V_HOMES)
    z_chip = pick_homes([down_load, up_load], 12000, Z_HOMES)

    def make_rounds(chip_of, seed):
        flows = [
            (chip_of[tile * units + unit], d, role * units + unit)
            for d in range(count)
            for role, tile in enumerate(pairs[d])
            for unit in range(units)
        ]
        return color_flows(flows, chips, count, hops, seed)

    def even(rounds, upward, seed):
        return even_rounds(rounds, chips, routes, n_links, upward, 6000, seed)

    v_rounds = make_rounds(v_chip, V_ROUNDS)
    z_rounds = even(make_rounds(z_chip, Z_ROUNDS), False, Z_ROUNDS)
    up_rounds = even(make_rounds(z_chip, Z_ROUNDS), True, Z_ROUNDS)
    n_rounds = len(z_rounds)
    second = {cores[1] for cores in chips}
    slot_table = np.zeros((count, 4 * n_rounds), np.int32)
    for r in range(n_rounds):
        for core, member, slot in v_rounds[r]:
            turn = int(core in second)
            slot_table[member, 2 * r:2 * r + 2] = (2 * slot + turn, 2 * slot + 1 - turn)
        for _, member, slot in z_rounds[r]:
            slot_table[member, 2 * n_rounds + r] = slot
        for _, member, slot in up_rounds[r]:
            slot_table[member, 3 * n_rounds + r] = slot
    v_down = [[(core, member) for core, member, _ in part] for part in v_rounds]
    z_down = [[(core, member) for core, member, _ in part] for part in z_rounds]
    up = [[(member, core) for core, member, _ in part] for part in up_rounds]
    settle = [(2 * u + c, chips[v_chip[u]][c]) for u in range(n_units) for c in range(2)]
    swap = [pair for a, b in chips for pair in ((a, b), (b, a))]
    far_perm = [
        (h * grid + k + h, h * grid + k) for h in range(half) for k in range(h)
    ]

    def send(value, perm):
        return lax.ppermute(value, AXES, perm)

    gaps = [2**i for i in range(count.bit_length() - 1)]
    gaps.sort(key=lambda gap: -hops[0, gap])

    def all_sum(value):
        for gap in gaps:
            value = value + send(value, [(d, d ^ gap) for d in range(count)])
        return value

    def body(matrix, far_diag, vectors, factors):
        tile = matrix.shape[0]
        rows, nb = vectors.shape
        step = next(n for n in (256, 128, tile) if tile % n == 0)
        row_at = lax.axis_index("row")
        col_at = lax.axis_index("col")
        me = row_at * grid + col_at
        table = lax.dynamic_slice_in_dim(jnp.asarray(slot_table), me, 1, 0)[0]
        v_slots, slots = table[:2 * n_rounds], table[2 * n_rounds:3 * n_rounds]
        up_slots = table[3 * n_rounds:]
        flags = jnp.stack(
            [(col_at == row_at).astype(jnp.int32), (col_at == row_at).astype(jnp.int32)]
        )
        v_first = send(vectors, settle)
        v_home = jnp.concatenate([v_first, send(v_first, swap)], axis=0)
        v_in = [send(v_home, perm) for perm in v_down]
        smem = pl.BlockSpec(memory_space=pltpu.SMEM)
        vmem = pl.BlockSpec(memory_space=pltpu.VMEM)
        unit = 2 * rows
        piece = jax.ShapeDtypeStruct((unit, nb), F32)

        hbm = pl.BlockSpec(memory_space=pltpu.HBM)
        keep = lambda value: pltpu.with_memory_space_constraint(value, pltpu.VMEM)
        cost = pl.CostEstimate(flops=4 * tile * tile, bytes_accessed=8 * tile * tile, transcendentals=0)
        copies = pltpu.SemaphoreType.DMA((tile // step,))
        high, low = pl.pallas_call(
            functools.partial(split_kernel, step),
            out_shape=[pltpu.MemorySpace.VMEM((tile, tile), BF16)] * 2,
            in_specs=[hbm],
            out_specs=[vmem] * 2,
            scratch_shapes=[pltpu.VMEM((tile, tile), F32), copies],
            compiler_params=pltpu.CompilerParams(vmem_limit_bytes=12 * 2**20),
            cost_estimate=cost,
            name="split_block",
        )(matrix)
        block = pl.pallas_call(
            functools.partial(load_kernel, step),
            out_shape=pltpu.MemorySpace.VMEM((tile, tile), F32),
            in_specs=[hbm],
            out_specs=vmem,
            scratch_shapes=[copies],
            compiler_params=pltpu.CompilerParams(vmem_limit_bytes=4 * 2**20),
            cost_estimate=cost,
            name="load_block",
        )(matrix)
        outs = pl.pallas_call(
            functools.partial(z_kernel, n_rounds, step),
            out_shape=[piece] * n_rounds + [jax.ShapeDtypeStruct((nb, nb), F32)],
            in_specs=[smem] * 3 + [vmem] * (3 + n_rounds),
            out_specs=[vmem] * (n_rounds + 1),
            scratch_shapes=[
                pltpu.VMEM((2, tile, nb), F32),
                pltpu.VMEM((2, tile, 2 * nb), BF16),
                pltpu.VMEM((2, 2 * nb, tile), BF16),
                pltpu.VMEM((2, tile, nb), F32),
                pltpu.VMEM((2, 2 * nb, tile), F32),
            ],
            compiler_params=pltpu.CompilerParams(vmem_limit_bytes=20 * 2**20),
            name="z_block",
        )(v_slots, up_slots, flags, keep(high), keep(low), far_diag, *v_in)
        z_parts, g_part = outs[:n_rounds], outs[n_rounds]

        z_here = [send(z_parts[r], perm) for r, perm in enumerate(up)]
        gram = all_sum(g_part)
        z_sum = functools.reduce(lambda a, b: a + b, z_here)
        z_home = z_sum + send(z_sum, swap)
        z_in = [send(z_home, perm) for perm in z_down]

        hi, lo, far_own = pl.pallas_call(
            functools.partial(w_kernel, n_rounds),
            out_shape=[
                jax.ShapeDtypeStruct((2, tile, 2 * nb), BF16),
                jax.ShapeDtypeStruct((2, tile, 2 * nb), BF16),
                jax.ShapeDtypeStruct((1, tile), F32),
            ],
            in_specs=[smem] * 3 + [vmem] * (3 + 2 * n_rounds),
            out_specs=[vmem] * 3,
            scratch_shapes=[pltpu.VMEM((2, tile, nb), F32), pltpu.VMEM((2, tile, nb), F32)],
            compiler_params=pltpu.CompilerParams(vmem_limit_bytes=16 * 2**20),
            name="w_block",
        )(v_slots, slots, flags, gram, factors, far_diag, *v_in, *z_in)
        far_sent = lax.ppermute(far_own, AXES, far_perm)

        updated = pl.pallas_call(
            functools.partial(u_kernel, step),
            out_shape=jax.ShapeDtypeStruct((tile, tile), F32),
            in_specs=[smem, vmem, vmem, vmem],
            out_specs=pl.BlockSpec(memory_space=pl.ANY),
            scratch_shapes=[pltpu.VMEM((tile, tile), F32), pltpu.SemaphoreType.DMA((tile // step,))],
            compiler_params=pltpu.CompilerParams(vmem_limit_bytes=20 * 2**20),
            cost_estimate=pl.CostEstimate(
                flops=12 * tile * tile * nb, bytes_accessed=8 * tile * tile, transcendentals=0
            ),
            name="u_block",
        )(flags, keep(block), hi, lo)
        far_updated = jnp.where(col_at < row_at, far_sent, far_own)
        return updated, far_updated

    in_specs = (P("row", "col"), P("row", None), P(AXES, None), P())
    out_specs = (P("row", "col"), P("row", None))
    return jax.shard_map(body, mesh=mesh, in_specs=in_specs, out_specs=out_specs, check_vma=False)
```
